32 devices in a mesh: row: 4 (over y, x), col: 8 (over z, core).
Axes of the slice: x: 2, y: 2, z: 4, core: 2. Of those that a mesh axis runs over, the one named last changes fastest.
Arguments:
- legendre: bfloat16 [512, 512, 512], P('row', 'col'), may hold values from -6 to 6
- vectors: bfloat16 [512, 512, 256], P('row', 'col'), may hold values from -6 to 6
- panel_orders: int32 [4], replicated, may hold values from 0 to 511, as said below
- cycle_span: int32 [512, 2], replicated, may hold values from 0 to 2047, as said below
- cycle_weight: float32 [512], replicated, may hold values from 0.0009765625 to 0.0029296875
Outputs:
- projected: bfloat16 [512, 4, 256], P('col', 'row')
The draws below stay inside these ranges and needn't reach their ends.
Inputs may be any that keep to these rules, and one draw needn't show every extreme that they name: `panel_orders`: the 4 entries are distinct orders; 0 and 511 are among them. `cycle_span`: in every cycle the first entry is smaller than the second.
All inputs are finite; a program needn't handle non-finite values.
Results may differ from the reference program's by a relative error of at most 0.008.
Values may be sent and summed in bfloat16 or wider, within the bound.
A program may use at most 64 MiB of HBM per device.

```python
import math
import jax
import jax.numpy as jnp
from jax import lax

BAND = 512
CYCLES = 512
VECS = 256
NPHI = 2048
PANEL = 4


def draw_panel_orders(key, part):
    inner = jax.random.permutation(jax.random.fold_in(key, 11), BAND - 2) + 1
    chosen = jnp.concatenate([jnp.array([0, BAND - 1], dtype=jnp.int32), inner[:PANEL - 2].astype(jnp.int32)])
    return jax.random.permutation(jax.random.fold_in(key, 13), chosen).astype(jnp.int32)


def draw_cycle_span(key, part):
    start_key, width_key = jax.random.split(jax.random.fold_in(key, 23))
    span_start = jax.random.randint(start_key, (CYCLES,), 0, NPHI // 2)
    span_width = jax.random.randint(width_key, (CYCLES,), NPHI // 16, NPHI // 2)
    return jnp.stack([span_start, span_start + span_width], axis=1).astype(jnp.int32)


def steps_of(rng, shape, cuts, low, high):
    loudness, own = 1.0, jax.random.fold_in(rng, 6)
    for dim, shards_of in cuts:
        steps = jnp.exp(jax.random.uniform(jax.random.fold_in(own, dim), (shards_of,), jnp.float32, low / len(cuts), high / len(cuts)))
        loudness = loudness * jnp.repeat(steps, shape[dim] // shards_of).reshape([-1 if axis == dim else 1 for axis in range(len(shape))])
    return loudness


def noise(key, dims, spread, reach, pieces=(), kind=jnp.bfloat16):
    gain = steps_of(key, dims, pieces, -0.22, 0.18) if pieces else 1.0
    drawn = jax.random.normal(key, dims, jnp.float32) * spread * gain
    return jnp.minimum(jnp.maximum(drawn, -reach), reach).astype(kind)


def setup_inputs(seed: int = 0) -> dict:
    keys = jax.random.split(jax.random.key(seed), 6)
    legendre = noise(keys[0], (BAND, BAND, CYCLES), 1.0, 6.0, ((0, 4), (1, 8)))
    vectors = noise(keys[1], (BAND, BAND, VECS), 1.0, 6.0, ((0, 4), (1, 8)))
    panel_orders = draw_panel_orders(jax.random.fold_in(keys[5], 71), 0)
    cycle_span = draw_cycle_span(jax.random.fold_in(keys[5], 71), 0)
    cycle_weight = jnp.clip(jax.random.uniform(keys[4], (CYCLES,), jnp.float32, 0.0009765625, 0.0029296875), 0.0009765625, 0.0029296875)
    return dict(legendre=legendre, vectors=vectors, panel_orders=panel_orders, cycle_span=cycle_span, cycle_weight=cycle_weight)


def mask_coef(wavenumber, span_start, span_stop):
    cell_angle = 2.0 * math.pi / NPHI
    upper_sine = jnp.sin(cell_angle * ((wavenumber * span_stop) % NPHI).astype(jnp.float32))
    lower_sine = jnp.sin(cell_angle * ((wavenumber * span_start) % NPHI).astype(jnp.float32))
    half_angle = 2.0 * jnp.sin((math.pi / NPHI) * wavenumber.astype(jnp.float32))
    safe_denom = jnp.where(wavenumber == 0, jnp.ones_like(half_angle), half_angle)
    span_width = cell_angle * (span_stop - span_start).astype(jnp.float32)
    return jnp.where(wavenumber == 0, span_width, cell_angle * (upper_sine - lower_sine) / safe_denom)


def cycle_mix(first_orders, col_orders, cycle_span, cycle_weight):
    span_start = cycle_span[:, 0][None, None, :]
    span_stop = cycle_span[:, 1][None, None, :]
    order_gap = jnp.abs(first_orders[:, None] - col_orders[None, :])[:, :, None]
    order_sum = (first_orders[:, None] + col_orders[None, :])[:, :, None]
    coef_sum = mask_coef(order_gap, span_start, span_stop) + mask_coef(order_sum, span_start, span_stop)
    return 0.5 * cycle_weight[None, None, :] * coef_sum


def reference(legendre, vectors, panel_orders, cycle_span, cycle_weight):
    orders = jnp.arange(BAND, dtype=jnp.int32)
    keep_mask = orders[None, :] >= orders[:, None]
    tables = jnp.where(keep_mask[:, :, None], legendre, jnp.zeros((), jnp.bfloat16))
    panel_rows = tables[panel_orders].astype(jnp.float32)
    mix_coef = cycle_mix(panel_orders, orders, cycle_span, cycle_weight)
    order_block = 8

    def add_block(block_index, running):
        block_start = (block_index * order_block).astype(jnp.int32)
        col_tables = lax.dynamic_slice_in_dim(tables, block_start, order_block, 0)
        cycle_coef = lax.dynamic_slice_in_dim(mix_coef, block_start, order_block, 1)
        vec_block = lax.dynamic_slice_in_dim(vectors, block_start, order_block, 0)
        vec_block = vec_block.reshape(order_block * BAND, VECS).astype(jnp.float32)
        weighted = (cycle_coef[:, :, None, :] * col_tables[None].astype(jnp.float32)).astype(jnp.bfloat16)
        weighted = weighted.reshape(PANEL, order_block * BAND, CYCLES).astype(jnp.float32)
        panel_block = jnp.einsum('plj,pqj->plq', panel_rows, weighted).astype(jnp.bfloat16)
        return running + jnp.einsum('plq,qk->lpk', panel_block.astype(jnp.float32), vec_block)

    initial = jnp.zeros((BAND, PANEL, VECS), jnp.float32)
    running = lax.fori_loop(0, BAND // order_block, add_block, initial)
    return running.astype(jnp.bfloat16)
```

```python
import functools
import math

import jax
import jax.numpy as jnp
from jax import lax
from jax.experimental import pallas as pl
from jax.experimental.pallas import tpu as pltpu
from jax.sharding import PartitionSpec as P

NPHI = 2048
MESH = pl.DeviceIdType.MESH
BF16 = jnp.bfloat16
F32 = jnp.float32


def sine_pair(orders, cells):
    angle = (2.0 * math.pi / NPHI) * (orders[:, None] * cells[None, :] % NPHI).astype(F32)
    return jnp.sin(angle), jnp.cos(angle)


def order_sines(first_order, ord_count, cells):
    step = 16
    high_sin, high_cos = sine_pair(first_order + step * jnp.arange(ord_count // step, dtype=jnp.int32), cells)
    low_sin, low_cos = sine_pair(jnp.arange(step, dtype=jnp.int32), cells)
    high_sin, high_cos = high_sin[:, None], high_cos[:, None]
    low_sin, low_cos = low_sin[None], low_cos[None]
    shape = (ord_count, cells.shape[0])
    sines = (high_sin * low_cos + high_cos * low_sin).reshape(shape)
    cosines = (high_cos * low_cos - high_sin * low_sin).reshape(shape)
    return sines, cosines


def inverse_chord(wavenumber):
    chord = 2.0 * jnp.sin((math.pi / NPHI) * wavenumber.astype(F32))
    zero = wavenumber == 0
    return jnp.where(zero, 0.0, 1.0 / jnp.where(zero, 1.0, chord))


def cycle_mix(panel_orders, first_order, ord_count, cycle_span, cycle_weight):
    cell_angle = 2.0 * math.pi / NPHI
    start, stop = cycle_span[:, 0], cycle_span[:, 1]
    orders = first_order + jnp.arange(ord_count, dtype=jnp.int32)
    stop_sin, stop_cos = order_sines(first_order, ord_count, stop)
    start_sin, start_cos = order_sines(first_order, ord_count, start)
    pan_stop_sin, pan_stop_cos = sine_pair(panel_orders, stop)
    pan_start_sin, pan_start_cos = sine_pair(panel_orders, start)
    gap = panel_orders[:, None] - orders[None, :]
    total = panel_orders[:, None] + orders[None, :]
    gap_inv, sum_inv = inverse_chord(gap), inverse_chord(total)
    zeros = (gap == 0).astype(F32) + (total == 0).astype(F32)
    even = pan_stop_sin[:, None] * stop_cos[None] - pan_start_sin[:, None] * start_cos[None]
    odd = pan_stop_cos[:, None] * stop_sin[None] - pan_start_cos[:, None] * start_sin[None]
    width = (stop - start).astype(F32)
    mixed = (
        even * (sum_inv + gap_inv)[:, :, None]
        + odd * (sum_inv - gap_inv)[:, :, None]
        + zeros[:, :, None] * width[None, None, :]
    )
    return (0.5 * cell_angle) * cycle_weight[None, None, :] * mixed


def kernel(
    rows, cols, chunk,
    t_hbm, v_hbm, coef_ref, keep_ref, pick_ref, out_ref,
    tbuf, vbuf, vt, acc, own, half_send, half_recv, row_send, row_recv,
    pick_recv, tm, op_send, op_recv, fin_send, fin_recv,
    in_sem, half_ss, half_rs, row_ss, row_rs, pick_ss, pick_rs,
    tmz_ss, tmz_rs, tmp_ss, tmp_rs, op_ss, op_rs, fin_ss, fin_rs,
):
    r = lax.axis_index("row")
    c = lax.axis_index("col")
    groups = cols // 2
    core = c % 2
    group = c // 2
    partner = group * 2 + 1 - core
    ords, degs, cyc = tbuf.shape
    vecs = vbuf.shape[2]
    half = vecs // 2
    n_chunks = ords // chunk
    depth = chunk * degs

    loads = []
    for i in range(n_chunks):
        piece = pl.ds(i * chunk, chunk)
        loads.append((
            pltpu.make_async_copy(t_hbm.at[piece], tbuf.at[piece], in_sem.at[0, i]),
            pltpu.make_async_copy(v_hbm.at[piece], vbuf.at[piece], in_sem.at[1, i]),
        ))
        loads[-1][0].start()
        loads[-1][1].start()

    barrier = pltpu.get_barrier_semaphore()
    pl.semaphore_signal(barrier, inc=1, device_id=(r, partner), device_id_type=MESH)
    for s in range(1, rows):
        pl.semaphore_signal(barrier, inc=1, device_id=((r + s) % rows, c), device_id_type=MESH)
    for i in range(1, groups):
        pl.semaphore_signal(
            barrier, inc=1, device_id=(r, ((group + i) % groups) * 2 + core), device_id_type=MESH
        )
    pl.semaphore_wait(barrier, 1 + (rows - 1) + (groups - 1))

    def remote(src, dst, ss, rs, dev):
        copy = pltpu.make_async_remote_copy(
            src_ref=src, dst_ref=dst, send_sem=ss, recv_sem=rs, device_id=dev, device_id_type=MESH
        )
        copy.start()
        return copy

    picks = [
        remote(pick_ref.at[(r + s) % rows], pick_recv.at[s - 1], pick_ss.at[s - 1], pick_rs.at[s - 1],
               ((r + s) % rows, c))
        for s in range(1, rows)
    ]

    def scaled(panel, i):
        terms = []
        for o in range(chunk):
            index = i * chunk + o
            scale = jnp.broadcast_to(coef_ref[panel, pl.ds(index, 1), :], (16, cyc)).astype(BF16)
            block = tbuf[index].reshape(degs // 16, 16, cyc) * scale[None]
            terms.append(block.reshape(degs, cyc))
        return jnp.concatenate(terms, axis=0)

    def phase(panel, first):
        acc[...] = jnp.zeros_like(acc)
        if first:
            for i in range(n_chunks):
                loads[i][0].wait()
                loads[i][1].wait()
                span = slice(i * depth, (i + 1) * depth)
                block = vbuf[i * chunk:(i + 1) * chunk].reshape(depth, vecs)
                turned = block.T * jnp.broadcast_to(keep_ref[:, span], (16, depth)).astype(BF16)[:1]
                vt[:, span] = turned
                acc[...] += jnp.dot(turned, scaled(panel, i), preferred_element_type=F32)
        else:
            @pl.loop(0, n_chunks)
            def _(i):
                left = vt[:, pl.ds(pl.multiple_of(i * depth, depth), depth)]
                acc[...] += jnp.dot(left, scaled(panel, i), preferred_element_type=F32)

    mine = pl.ds(pl.multiple_of(core * half, half), half)
    other = pl.ds(pl.multiple_of((1 - core) * half, half), half)
    halves = []
    rowed = []

    def send_half(s):
        own[s] = acc[mine, :]
        half_send[s] = acc[other, :].astype(BF16)
        halves.append(remote(half_send.at[s], half_recv.at[s], half_ss.at[s], half_rs.at[s], (r, partner)))

    def send_row(s):
        halves[s].wait()
        row_send[s] = (own[s] + half_recv[s].astype(F32)).astype(BF16)
        rowed.append(remote(row_send.at[s], row_recv.at[s], row_ss.at[s], row_rs.at[s], ((r + s + 1) % rows, c)))

    later = []
    for s in range(rows):
        phase((r + s + 1) % rows, s == 0)
        send_half(s)
        if s == 0:
            for copy in picks:
                copy.wait()
            found = pick_ref[r].astype(F32)
            for q in range(rows - 1):
                found = found + pick_recv[q].astype(F32)
            tm[c] = found.astype(BF16)
            later = [
                remote(tm.at[c], tm.at[c], tmz_ss.at[i - 1], tmz_rs.at[i - 1],
                       (r, ((group + i) % groups) * 2 + core))
                for i in range(1, groups)
            ]
            later_core = [remote(tm.at[c], tm.at[c], tmp_ss.at[0], tmp_rs.at[0], (r, partner))]
        else:
            send_row(s - 1)
        if s == 1:
            for i in range(1, groups):
                later[i - 1].wait()
                came = ((group - i + groups) % groups) * 2 + core
                later_core.append(
                    remote(tm.at[came], tm.at[came], tmp_ss.at[i], tmp_rs.at[i], (r, partner))
                )
    for copy in later_core:
        copy.wait()
    halves[rows - 1].wait()
    summed = own[rows - 1] + half_recv[rows - 1].astype(F32)
    for s in range(rows - 1):
        rowed[s].wait()
        summed = summed + row_recv[s].astype(F32)
    summed = summed.astype(BF16)
    table = tm[...].reshape(cols * degs, cyc)
    product = lax.dot_general(table, summed, (((1,), (1,)), ((), ())), preferred_element_type=F32)
    op_send[...] = product.astype(BF16).reshape(groups, 2 * degs, half)
    sends = []
    for i in range(1, groups):
        to = (group + i) % groups
        sends.append(
            remote(op_send.at[to], op_recv.at[i - 1], op_ss.at[i - 1], op_rs.at[i - 1], (r, to * 2 + core))
        )
    total = op_send[group].astype(F32)
    for i in range(1, groups):
        sends[i - 1].wait()
        total = total + op_recv[i - 1].astype(F32)
    own[0, :2 * degs, :half] = total
    near = own[0, pl.ds(pl.multiple_of(core * degs, degs), degs), :half]
    far = own[0, pl.ds(pl.multiple_of((1 - core) * degs, degs), degs), :half]
    fin_send[...] = far.astype(BF16)
    last = remote(fin_send, fin_recv, fin_ss, fin_rs, (r, partner))
    out_ref[:, mine] = near.astype(BF16)
    last.wait()
    out_ref[:, other] = fin_recv[...]


def per_device(rows, cols, legendre, vectors, panel_orders, cycle_span, cycle_weight):
    ords, degs, cyc = legendre.shape
    vecs = vectors.shape[2]
    panels = panel_orders.shape[0]
    assert panels == rows
    first_order = lax.axis_index("row") * ords
    first_degree = lax.axis_index("col") * degs
    local_orders = first_order + jnp.arange(ords, dtype=jnp.int32)
    local_degrees = first_degree + jnp.arange(degs, dtype=jnp.int32)
    keep = (local_degrees[None, :] >= local_orders[:, None]).astype(F32).reshape(1, ords * degs)
    coef = cycle_mix(panel_orders, first_order, ords, cycle_span, cycle_weight)
    place = jnp.clip(panel_orders - first_order, 0, ords - 1)
    held = (panel_orders >= first_order) & (panel_orders < first_order + ords)
    held = held[:, None] & (local_degrees[None, :] >= panel_orders[:, None])
    picked = jnp.concatenate(
        [lax.dynamic_slice_in_dim(legendre, place[p], 1, 0) for p in range(panels)], axis=0
    )
    picked = jnp.where(held[:, :, None], picked, jnp.zeros((), BF16))

    groups, half = cols // 2, vecs // 2
    chunk = 8
    while ords % chunk or (chunk * degs) % 128:
        chunk *= 2
    dma = pltpu.SemaphoreType.DMA
    vmem = pl.BlockSpec(memory_space=pltpu.VMEM)
    hbm = pl.BlockSpec(memory_space=pl.ANY)
    return pl.pallas_call(
        functools.partial(kernel, rows, cols, chunk),
        out_shape=jax.ShapeDtypeStruct((degs, vecs), BF16),
        in_specs=[hbm, hbm, vmem, vmem, vmem],
        out_specs=vmem,
        scratch_shapes=[
            pltpu.VMEM((ords, degs, cyc), BF16),
            pltpu.VMEM((ords, degs, vecs), BF16),
            pltpu.VMEM((vecs, ords * degs), BF16),
            pltpu.VMEM((vecs, cyc), F32),
            pltpu.VMEM((rows, half, cyc), F32),
            pltpu.VMEM((rows, half, cyc), BF16),
            pltpu.VMEM((rows, half, cyc), BF16),
            pltpu.VMEM((rows - 1, half, cyc), BF16),
            pltpu.VMEM((rows - 1, half, cyc), BF16),
            pltpu.VMEM((rows - 1, degs, cyc), BF16),
            pltpu.VMEM((cols, degs, cyc), BF16),
            pltpu.VMEM((groups, 2 * degs, half), BF16),
            pltpu.VMEM((groups - 1, 2 * degs, half), BF16),
            pltpu.VMEM((degs, half), BF16),
            pltpu.VMEM((degs, half), BF16),
            dma((2, ords // chunk)),
            dma((rows,)), dma((rows,)),
            dma((rows - 1,)), dma((rows - 1,)),
            dma((rows - 1,)), dma((rows - 1,)),
            dma((groups - 1,)), dma((groups - 1,)),
            dma((groups,)), dma((groups,)),
            dma((groups - 1,)), dma((groups - 1,)),
            dma, dma,
        ],
        compiler_params=pltpu.CompilerParams(
            collective_id=0, has_side_effects=True, vmem_limit_bytes=60 * 1024 * 1024
        ),
    )(legendre, vectors, coef, keep, picked)


def solution(mesh):
    rows, cols = mesh.shape["row"], mesh.shape["col"]

    def body(*args):
        return per_device(rows, cols, *args)[:, None, :]

    in_specs = (P("row", "col", None), P("row", "col", None), P(), P(), P())
    return jax.shard_map(
        body, mesh=mesh, in_specs=in_specs, out_specs=P("col", "row", None), check_vma=False
    )
```

```python
import functools
import math

import jax
import jax.numpy as jnp
from jax import lax
from jax.experimental import pallas as pl
from jax.experimental.pallas import tpu as pltpu
from jax.sharding import PartitionSpec as P

NPHI = 2048
MESH = pl.DeviceIdType.MESH
BF16 = jnp.bfloat16
F32 = jnp.float32


def sine_pair(orders, cells):
    angle = (2.0 * math.pi / NPHI) * ((orders * cells) & (NPHI - 1)).astype(F32)
    return jnp.sin(angle), jnp.cos(angle)


def cycle_mix(order_of, panels, first_order, span, weight, coef_ref):
    ords, cyc = coef_ref.shape[1:]
    step = 16
    cell_angle = 2.0 * math.pi / NPHI
    start, stop = span[0:1, :], span[1:2, :]
    scale = (0.5 * cell_angle) * weight
    width = scale * (stop - start).astype(F32)
    low = lax.broadcasted_iota(jnp.int32, (step, cyc), 0)
    high_count = ords // step
    high = first_order + step * lax.broadcasted_iota(jnp.int32, (high_count, cyc), 0)
    low_stop, low_start = sine_pair(low, stop), sine_pair(low, start)
    high_stop, high_start = sine_pair(high, stop), sine_pair(high, start)
    ident = lax.broadcasted_iota(jnp.int32, (panels, cyc), 0)
    pan = jnp.zeros((panels, cyc), jnp.int32)
    for p in range(panels):
        pan = jnp.where(ident == p, order_of[p], pan)
    pan_stop = [scale * x for x in sine_pair(pan, stop)]
    pan_start = [scale * x for x in sine_pair(pan, start)]
    lane = lax.broadcasted_iota(jnp.int32, (ords, 128), 1)
    order = first_order + lax.broadcasted_iota(jnp.int32, (ords, 128), 0)
    wave = jnp.ones((ords, 128), jnp.int32)
    for p in range(panels):
        wave = jnp.where(lane == 2 * p, order_of[p] - order, wave)
        wave = jnp.where(lane == 2 * p + 1, order_of[p] + order, wave)
    zero = wave == 0
    chord = 2.0 * jnp.sin((math.pi / NPHI) * wave.astype(F32))
    inverse = jnp.where(zero, 0.0, 1.0 / jnp.where(zero, 1.0, chord))
    zeros = zero.astype(F32)
    for a in range(high_count):
        rows = slice(a * step, (a + 1) * step)

        def turned(high_pair, low_pair):
            hs, hc = high_pair[0][a:a + 1], high_pair[1][a:a + 1]
            return hs * low_pair[1] + hc * low_pair[0], hc * low_pair[1] - hs * low_pair[0]

        stop_sin, stop_cos = turned(high_stop, low_stop)
        start_sin, start_cos = turned(high_start, low_start)
        for p in range(panels):
            one = slice(p, p + 1)
            even = pan_stop[0][one] * stop_cos - pan_start[0][one] * start_cos
            odd = pan_stop[1][one] * stop_sin - pan_start[1][one] * start_sin
            gap, total = inverse[rows, 2 * p:2 * p + 1], inverse[rows, 2 * p + 1:2 * p + 2]
            flat = zeros[rows, 2 * p:2 * p + 1] + zeros[rows, 2 * p + 1:2 * p + 2]
            coef_ref[p, rows, :] = even * (total + gap) + odd * (total - gap) + flat * width


def kernel(
    rows, cols, chunk,
    t_hbm, v_hbm, order_ref, span_ref, weight_ref, out_ref,
    coef_ref, pick_ref, tbuf, vbuf, vt, acc, own, half_send, half_recv, row_send, row_recv,
    pick_recv, tm, op_send, op_recv, fin_send, fin_recv,
    in_sem, half_ss, half_rs, row_ss, row_rs, pick_ss, pick_rs,
    tmz_ss, tmz_rs, tmp_ss, tmp_rs, op_ss, op_rs, fin_ss, fin_rs,
):
    r = lax.axis_index("row")
    c = lax.axis_index("col")
    groups = cols // 2
    core = c % 2
    group = c // 2
    partner = group * 2 + 1 - core
    ords, degs, cyc = tbuf.shape
    vecs = vbuf.shape[2]
    half = vecs // 2
    n_chunks = ords // chunk
    depth = chunk * degs

    loads = []
    for i in range(n_chunks):
        piece = pl.ds(i * chunk, chunk)
        loads.append((
            pltpu.make_async_copy(t_hbm.at[piece], tbuf.at[piece], in_sem.at[0, i]),
            pltpu.make_async_copy(v_hbm.at[piece], vbuf.at[piece], in_sem.at[1, i]),
        ))
        loads[-1][0].start()
        loads[-1][1].start()

    barrier = pltpu.get_barrier_semaphore()
    pl.semaphore_signal(barrier, inc=1, device_id=(r, partner), device_id_type=MESH)
    for s in range(1, rows):
        pl.semaphore_signal(barrier, inc=1, device_id=((r + s) % rows, c), device_id_type=MESH)
    for i in range(1, groups):
        pl.semaphore_signal(
            barrier, inc=1, device_id=(r, ((group + i) % groups) * 2 + core), device_id_type=MESH
        )
    pl.semaphore_wait(barrier, 1 + (rows - 1) + (groups - 1))

    def remote(src, dst, ss, rs, dev):
        copy = pltpu.make_async_remote_copy(
            src_ref=src, dst_ref=dst, send_sem=ss, recv_sem=rs, device_id=dev, device_id_type=MESH
        )
        copy.start()
        return copy

    panels = rows
    first_order, first_degree = r * ords, c * degs
    order_of = [order_ref[p] for p in range(panels)]
    cycle_mix(order_of, panels, first_order, span_ref[...], weight_ref[...], coef_ref)

    def kept(i):
        index = i * depth + lax.broadcasted_iota(jnp.int32, (16, depth), 1)
        shift = degs.bit_length() - 1
        order = first_order + lax.shift_right_logical(index, shift)
        degree = first_degree + (index & (degs - 1))
        return jnp.where(degree >= order, 1.0, 0.0).astype(BF16)[:1]

    def pick(p):
        place = jnp.clip(order_of[p] - first_order, 0, ords - 1)
        held = (order_of[p] >= first_order) & (order_of[p] < first_order + ords)
        degree = first_degree + lax.broadcasted_iota(jnp.int32, (degs, cyc), 0)
        keep = (degree >= order_of[p]) & held
        pick_ref[p] = jnp.where(keep, tbuf[place].astype(F32), 0.0).astype(BF16)

    def scaled(panel, i):
        terms = []
        for o in range(chunk):
            index = i * chunk + o
            scale = jnp.broadcast_to(coef_ref[panel, pl.ds(index, 1), :], (16, cyc)).astype(BF16)
            block = tbuf[index].reshape(degs // 16, 16, cyc) * scale[None]
            terms.append(block.reshape(degs, cyc))
        return jnp.concatenate(terms, axis=0)

    def phase(panel, first):
        acc[...] = jnp.zeros_like(acc)
        if first:
            for i in range(n_chunks):
                loads[i][0].wait()
                loads[i][1].wait()
                span = slice(i * depth, (i + 1) * depth)
                block = vbuf[i * chunk:(i + 1) * chunk].reshape(depth, vecs)
                turned = block.T * kept(i)
                vt[:, span] = turned
                acc[...] += jnp.dot(turned, scaled(panel, i), preferred_element_type=F32)
        else:
            @pl.loop(0, n_chunks)
            def _(i):
                left = vt[:, pl.ds(pl.multiple_of(i * depth, depth), depth)]
                acc[...] += jnp.dot(left, scaled(panel, i), preferred_element_type=F32)

    mine = pl.ds(pl.multiple_of(core * half, half), half)
    other = pl.ds(pl.multiple_of((1 - core) * half, half), half)
    halves = []
    rowed = []

    def send_half(s):
        own[s] = acc[mine, :]
        half_send[s] = acc[other, :].astype(BF16)
        halves.append(remote(half_send.at[s], half_recv.at[s], half_ss.at[s], half_rs.at[s], (r, partner)))

    def send_row(s):
        halves[s].wait()
        row_send[s] = (own[s] + half_recv[s].astype(F32)).astype(BF16)
        rowed.append(remote(row_send.at[s], row_recv.at[s], row_ss.at[s], row_rs.at[s], ((r + s + 1) % rows, c)))

    for s in range(rows):
        phase((r + s + 1) % rows, s == 0)
        send_half(s)
        if s == 0:
            for p in range(panels):
                pick(p)
            picks = [
                remote(pick_ref.at[(r + q) % rows], pick_recv.at[q - 1], pick_ss.at[q - 1],
                       pick_rs.at[q - 1], ((r + q) % rows, c))
                for q in range(1, rows)
            ]
        else:
            send_row(s - 1)
        if s == 1:
            for copy in picks:
                copy.wait()
            found = pick_ref[r].astype(F32)
            for q in range(rows - 1):
                found = found + pick_recv[q].astype(F32)
            tm[c] = found.astype(BF16)
            later = [
                remote(tm.at[c], tm.at[c], tmz_ss.at[i - 1], tmz_rs.at[i - 1],
                       (r, ((group + i) % groups) * 2 + core))
                for i in range(1, groups)
            ]
            later_core = [remote(tm.at[c], tm.at[c], tmp_ss.at[0], tmp_rs.at[0], (r, partner))]
        if s == 2:
            for i in range(1, groups):
                later[i - 1].wait()
                came = ((group - i + groups) % groups) * 2 + core
                later_core.append(
                    remote(tm.at[came], tm.at[came], tmp_ss.at[i], tmp_rs.at[i], (r, partner))
                )
    for copy in later_core:
        copy.wait()
    halves[rows - 1].wait()
    summed = own[rows - 1] + half_recv[rows - 1].astype(F32)
    for s in range(rows - 1):
        rowed[s].wait()
        summed = summed + row_recv[s].astype(F32)
    summed = summed.astype(BF16)
    table = tm[...].reshape(cols * degs, cyc)
    product = lax.dot_general(table, summed, (((1,), (1,)), ((), ())), preferred_element_type=F32)
    op_send[...] = product.astype(BF16).reshape(groups, 2 * degs, half)
    sends = []
    for i in range(1, groups):
        to = (group + i) % groups
        sends.append(
            remote(op_send.at[to], op_recv.at[i - 1], op_ss.at[i - 1], op_rs.at[i - 1], (r, to * 2 + core))
        )
    total = op_send[group].astype(F32)
    for i in range(1, groups):
        sends[i - 1].wait()
        total = total + op_recv[i - 1].astype(F32)
    own[0, :2 * degs, :half] = total
    near = own[0, pl.ds(pl.multiple_of(core * degs, degs), degs), :half]
    far = own[0, pl.ds(pl.multiple_of((1 - core) * degs, degs), degs), :half]
    fin_send[...] = far.astype(BF16)
    last = remote(fin_send, fin_recv, fin_ss, fin_rs, (r, partner))
    out_ref[:, mine] = near.astype(BF16)
    last.wait()
    out_ref[:, other] = fin_recv[...]


def per_device(rows, cols, legendre, vectors, panel_orders, cycle_span, cycle_weight):
    ords, degs, cyc = legendre.shape
    vecs = vectors.shape[2]
    panels = panel_orders.shape[0]
    assert panels == rows
    groups, half = cols // 2, vecs // 2
    chunk = 8
    while ords % chunk or (chunk * degs) % 128:
        chunk *= 2
    dma = pltpu.SemaphoreType.DMA
    vmem = pl.BlockSpec(memory_space=pltpu.VMEM)
    hbm = pl.BlockSpec(memory_space=pl.ANY)
    return pl.pallas_call(
        functools.partial(kernel, rows, cols, chunk),
        out_shape=jax.ShapeDtypeStruct((degs, vecs), BF16),
        in_specs=[hbm, hbm, pl.BlockSpec(memory_space=pltpu.SMEM), vmem, vmem],
        out_specs=vmem,
        scratch_shapes=[
            pltpu.VMEM((panels, ords, cyc), F32),
            pltpu.VMEM((panels, degs, cyc), BF16),
            pltpu.VMEM((ords, degs, cyc), BF16),
            pltpu.VMEM((ords, degs, vecs), BF16),
            pltpu.VMEM((vecs, ords * degs), BF16),
            pltpu.VMEM((vecs, cyc), F32),
            pltpu.VMEM((rows, half, cyc), F32),
            pltpu.VMEM((rows, half, cyc), BF16),
            pltpu.VMEM((rows, half, cyc), BF16),
            pltpu.VMEM((rows - 1, half, cyc), BF16),
            pltpu.VMEM((rows - 1, half, cyc), BF16),
            pltpu.VMEM((rows - 1, degs, cyc), BF16),
            pltpu.VMEM((cols, degs, cyc), BF16),
            pltpu.VMEM((groups, 2 * degs, half), BF16),
            pltpu.VMEM((groups - 1, 2 * degs, half), BF16),
            pltpu.VMEM((degs, half), BF16),
            pltpu.VMEM((degs, half), BF16),
            dma((2, ords // chunk)),
            dma((rows,)), dma((rows,)),
            dma((rows - 1,)), dma((rows - 1,)),
            dma((rows - 1,)), dma((rows - 1,)),
            dma((groups - 1,)), dma((groups - 1,)),
            dma((groups,)), dma((groups,)),
            dma((groups - 1,)), dma((groups - 1,)),
            dma, dma,
        ],
        compiler_params=pltpu.CompilerParams(
            collective_id=0, has_side_effects=True, vmem_limit_bytes=60 * 1024 * 1024
        ),
    )(legendre, vectors, panel_orders, cycle_span.T, cycle_weight[None, :])


def solution(mesh):
    rows, cols = mesh.shape["row"], mesh.shape["col"]

    def body(*args):
        return per_device(rows, cols, *args)[:, None, :]

    in_specs = (P("row", "col", None), P("row", "col", None), P(), P(), P())
    return jax.shard_map(
        body, mesh=mesh, in_specs=in_specs, out_specs=P("col", "row", None), check_vma=False
    )
```

```python
import functools
import math

import jax
import jax.numpy as jnp
from jax import lax
from jax.experimental import pallas as pl
from jax.experimental.pallas import tpu as pltpu
from jax.sharding import PartitionSpec as P

NPHI = 2048
MESH = pl.DeviceIdType.MESH
BF16 = jnp.bfloat16
F32 = jnp.float32


def sine_pair(orders, cells):
    angle = (2.0 * math.pi / NPHI) * ((orders * cells) & (NPHI - 1)).astype(F32)
    return jnp.sin(angle), jnp.cos(angle)


def cycle_mix(order_of, panels, first_order, span, weight, coef_ref):
    ords, cyc = coef_ref.shape[1:]
    step = 16
    cell_angle = 2.0 * math.pi / NPHI
    start, stop = span[0:1, :], span[1:2, :]
    scale = (0.5 * cell_angle) * weight
    width = scale * (stop - start).astype(F32)
    low = lax.broadcasted_iota(jnp.int32, (step, cyc), 0)
    high_count = ords // step
    high = first_order + step * lax.broadcasted_iota(jnp.int32, (high_count, cyc), 0)
    low_stop, low_start = sine_pair(low, stop), sine_pair(low, start)
    high_stop, high_start = sine_pair(high, stop), sine_pair(high, start)
    ident = lax.broadcasted_iota(jnp.int32, (panels, cyc), 0)
    pan = jnp.zeros((panels, cyc), jnp.int32)
    for p in range(panels):
        pan = jnp.where(ident == p, order_of[p], pan)
    pan_stop = [scale * x for x in sine_pair(pan, stop)]
    pan_start = [scale * x for x in sine_pair(pan, start)]
    lane = lax.broadcasted_iota(jnp.int32, (ords, 128), 1)
    order = first_order + lax.broadcasted_iota(jnp.int32, (ords, 128), 0)
    wave = jnp.ones((ords, 128), jnp.int32)
    for p in range(panels):
        wave = jnp.where(lane == 2 * p, order_of[p] - order, wave)
        wave = jnp.where(lane == 2 * p + 1, order_of[p] + order, wave)
    zero = wave == 0
    chord = 2.0 * jnp.sin((math.pi / NPHI) * wave.astype(F32))
    inverse = jnp.where(zero, 0.0, 1.0 / jnp.where(zero, 1.0, chord))
    zeros = zero.astype(F32)
    for a in range(high_count):
        rows = slice(a * step, (a + 1) * step)

        def turned(high_pair, low_pair):
            hs, hc = high_pair[0][a:a + 1], high_pair[1][a:a + 1]
            return hs * low_pair[1] + hc * low_pair[0], hc * low_pair[1] - hs * low_pair[0]

        stop_sin, stop_cos = turned(high_stop, low_stop)
        start_sin, start_cos = turned(high_start, low_start)
        for p in range(panels):
            one = slice(p, p + 1)
            even = pan_stop[0][one] * stop_cos - pan_start[0][one] * start_cos
            odd = pan_stop[1][one] * stop_sin - pan_start[1][one] * start_sin
            gap, total = inverse[rows, 2 * p:2 * p + 1], inverse[rows, 2 * p + 1:2 * p + 2]
            flat = zeros[rows, 2 * p:2 * p + 1] + zeros[rows, 2 * p + 1:2 * p + 2]
            coef_ref[p, rows, :] = even * (total + gap) + odd * (total - gap) + flat * width


def kernel(
    rows, cols, chunk,
    t_hbm, v_hbm, order_ref, span_ref, weight_ref, out_ref,
    coef_ref, pick_ref, tbuf, vbuf, vt, acc, own, half_send, half_recv, row_send, row_recv,
    pick_recv, tm, op_send, op_recv, fin_send, fin_recv,
    in_sem, half_ss, half_rs, row_ss, row_rs, pick_ss, pick_rs,
    tmz_ss, tmz_rs, tmp_ss, tmp_rs, op_ss, op_rs, fin_ss, fin_rs,
):
    r = lax.axis_index("row")
    c = lax.axis_index("col")
    groups = cols // 2
    core = c % 2
    group = c // 2
    partner = group * 2 + 1 - core
    ords, degs, cyc = tbuf.shape
    vecs = vbuf.shape[2]
    half = vecs // 2
    n_chunks = ords // chunk
    depth = chunk * degs

    loads = []
    for i in range(n_chunks):
        piece = pl.ds(i * chunk, chunk)
        loads.append((
            pltpu.make_async_copy(t_hbm.at[piece], tbuf.at[piece], in_sem.at[0, i]),
            pltpu.make_async_copy(v_hbm.at[piece], vbuf.at[piece], in_sem.at[1, i]),
        ))
        loads[-1][0].start()
        loads[-1][1].start()

    barrier = pltpu.get_barrier_semaphore()
    pl.semaphore_signal(barrier, inc=1, device_id=(r, partner), device_id_type=MESH)
    for s in range(1, rows):
        pl.semaphore_signal(barrier, inc=1, device_id=((r + s) % rows, c), device_id_type=MESH)
    for i in range(1, groups):
        pl.semaphore_signal(
            barrier, inc=1, device_id=(r, ((group + i) % groups) * 2 + core), device_id_type=MESH
        )
    pl.semaphore_wait(barrier, 1 + (rows - 1) + (groups - 1))

    def remote(src, dst, ss, rs, dev):
        copy = pltpu.make_async_remote_copy(
            src_ref=src, dst_ref=dst, send_sem=ss, recv_sem=rs, device_id=dev, device_id_type=MESH
        )
        copy.start()
        return copy

    panels = rows
    first_order, first_degree = r * ords, c * degs
    order_of = [order_ref[p] for p in range(panels)]
    cycle_mix(order_of, panels, first_order, span_ref[...], weight_ref[...], coef_ref)

    def kept(i):
        index = i * depth + lax.broadcasted_iota(jnp.int32, (16, depth), 1)
        shift = degs.bit_length() - 1
        order = first_order + lax.shift_right_logical(index, shift)
        degree = first_degree + (index & (degs - 1))
        return jnp.where(degree >= order, 1.0, 0.0).astype(BF16)[:1]

    def pick(p):
        place = jnp.clip(order_of[p] - first_order, 0, ords - 1)
        held = (order_of[p] >= first_order) & (order_of[p] < first_order + ords)
        degree = first_degree + lax.broadcasted_iota(jnp.int32, (degs, cyc), 0)
        keep = (degree >= order_of[p]) & held
        pick_ref[p] = jnp.where(keep, tbuf[place].astype(F32), 0.0).astype(BF16)

    def scaled(panel, start, count, span):
        width = cyc if span is None else cyc // 2
        span = slice(None) if span is None else span
        terms = []
        for o in range(count):
            index = start + o
            scale = jnp.broadcast_to(coef_ref[panel, pl.ds(index, 1), span], (16, width)).astype(BF16)
            block = tbuf[index, :, span].reshape(degs // 16, 16, width) * scale[None]
            terms.append(block.reshape(degs, width))
        return jnp.concatenate(terms, axis=0)

    def first_phase(panel):
        acc[...] = jnp.zeros_like(acc)
        for i in range(n_chunks):
            loads[i][0].wait()
            loads[i][1].wait()
            span = slice(i * depth, (i + 1) * depth)
            block = vbuf[i * chunk:(i + 1) * chunk].reshape(depth, vecs)
            turned = block.T * kept(i)
            vt[:, span] = turned
            acc[...] += jnp.dot(turned, scaled(panel, i * chunk, chunk, None), preferred_element_type=F32)

    def half_phase(panel, span):
        acc[:, span] = jnp.zeros((vecs, cyc // 2), F32)
        merge = 4 if ords % (4 * chunk) == 0 else 1
        large, long = merge * chunk, merge * depth

        @pl.loop(0, ords // large)
        def _(i):
            left = vt[:, pl.ds(pl.multiple_of(i * long, long), long)]
            acc[:, span] += jnp.dot(left, scaled(panel, i * large, large, span), preferred_element_type=F32)

    mine = pl.ds(pl.multiple_of(core * half, half), half)
    other = pl.ds(pl.multiple_of((1 - core) * half, half), half)
    halves = []
    rowed = []

    spans = (slice(0, cyc // 2), slice(cyc // 2, cyc))

    def send_half(s, span, sem):
        own[s, :, span] = acc[mine, span]
        half_send[s, :, span] = acc[other, span].astype(BF16)
        halves.append(
            remote(half_send.at[s, :, span], half_recv.at[s, :, span], half_ss.at[sem], half_rs.at[sem], (r, partner))
        )

    def send_row(s):
        halves[s].wait()
        row_send[s] = (own[s] + half_recv[s].astype(F32)).astype(BF16)
        rowed.append(remote(row_send.at[s], row_recv.at[s], row_ss.at[s], row_rs.at[s], ((r + s + 1) % rows, c)))

    for s in range(rows):
        panel = (r + s + 1) % rows
        if s == 0:
            first_phase(panel)
            send_half(0, slice(0, cyc), 0)
            for p in range(panels):
                pick(p)
            picks = [
                remote(pick_ref.at[(r + q) % rows], pick_recv.at[q - 1], pick_ss.at[q - 1],
                       pick_rs.at[q - 1], ((r + q) % rows, c))
                for q in range(1, rows)
            ]
            continue
        half_phase(panel, spans[0])
        send_row(s - 1)
        if s == rows - 1:
            send_half(s, spans[0], s)
        if s == 1:
            for copy in picks:
                copy.wait()
            found = pick_ref[r].astype(F32)
            for q in range(rows - 1):
                found = found + pick_recv[q].astype(F32)
            tm[c] = found.astype(BF16)
            later = [
                remote(tm.at[c], tm.at[c], tmz_ss.at[i - 1], tmz_rs.at[i - 1],
                       (r, ((group + i) % groups) * 2 + core))
                for i in range(1, groups)
            ]
            later_core = [remote(tm.at[c], tm.at[c], tmp_ss.at[0], tmp_rs.at[0], (r, partner))]
        half_phase(panel, spans[1])
        if s < rows - 1:
            send_half(s, slice(0, cyc), s)
        else:
            send_half(s, spans[1], s + 1)
        if s == 2:
            for i in range(1, groups):
                later[i - 1].wait()
                came = ((group - i + groups) % groups) * 2 + core
                later_core.append(
                    remote(tm.at[came], tm.at[came], tmp_ss.at[i], tmp_rs.at[i], (r, partner))
                )
    for copy in later_core:
        copy.wait()
    halves[rows - 1].wait()
    halves[rows].wait()
    summed = own[rows - 1] + half_recv[rows - 1].astype(F32)
    for s in range(rows - 1):
        rowed[s].wait()
        summed = summed + row_recv[s].astype(F32)
    summed = summed.astype(BF16)
    table = tm[...].reshape(cols * degs, cyc)
    product = lax.dot_general(table, summed, (((1,), (1,)), ((), ())), preferred_element_type=F32)
    op_send[...] = product.astype(BF16).reshape(groups, 2 * degs, half)
    sends = []
    for i in range(1, groups):
        to = (group + i) % groups
        sends.append(
            remote(op_send.at[to], op_recv.at[i - 1], op_ss.at[i - 1], op_rs.at[i - 1], (r, to * 2 + core))
        )
    total = op_send[group].astype(F32)
    for i in range(1, groups):
        sends[i - 1].wait()
        total = total + op_recv[i - 1].astype(F32)
    own[0, :2 * degs, :half] = total
    near = own[0, pl.ds(pl.multiple_of(core * degs, degs), degs), :half]
    far = own[0, pl.ds(pl.multiple_of((1 - core) * degs, degs), degs), :half]
    fin_send[...] = far.astype(BF16)
    last = remote(fin_send, fin_recv, fin_ss, fin_rs, (r, partner))
    out_ref[:, mine] = near.astype(BF16)
    last.wait()
    out_ref[:, other] = fin_recv[...]


def per_device(rows, cols, legendre, vectors, panel_orders, cycle_span, cycle_weight):
    ords, degs, cyc = legendre.shape
    vecs = vectors.shape[2]
    panels = panel_orders.shape[0]
    assert panels == rows
    groups, half = cols // 2, vecs // 2
    chunk = 8
    while ords % chunk or (chunk * degs) % 128:
        chunk *= 2
    dma = pltpu.SemaphoreType.DMA
    vmem = pl.BlockSpec(memory_space=pltpu.VMEM)
    hbm = pl.BlockSpec(memory_space=pl.ANY)
    return pl.pallas_call(
        functools.partial(kernel, rows, cols, chunk),
        out_shape=jax.ShapeDtypeStruct((degs, vecs), BF16),
        in_specs=[hbm, hbm, pl.BlockSpec(memory_space=pltpu.SMEM), vmem, vmem],
        out_specs=vmem,
        scratch_shapes=[
            pltpu.VMEM((panels, ords, cyc), F32),
            pltpu.VMEM((panels, degs, cyc), BF16),
            pltpu.VMEM((ords, degs, cyc), BF16),
            pltpu.VMEM((ords, degs, vecs), BF16),
            pltpu.VMEM((vecs, ords * degs), BF16),
            pltpu.VMEM((vecs, cyc), F32),
            pltpu.VMEM((rows, half, cyc), F32),
            pltpu.VMEM((rows, half, cyc), BF16),
            pltpu.VMEM((rows, half, cyc), BF16),
            pltpu.VMEM((rows - 1, half, cyc), BF16),
            pltpu.VMEM((rows - 1, half, cyc), BF16),
            pltpu.VMEM((rows - 1, degs, cyc), BF16),
            pltpu.VMEM((cols, degs, cyc), BF16),
            pltpu.VMEM((groups, 2 * degs, half), BF16),
            pltpu.VMEM((groups - 1, 2 * degs, half), BF16),
            pltpu.VMEM((degs, half), BF16),
            pltpu.VMEM((degs, half), BF16),
            dma((2, ords // chunk)),
            dma((rows + 1,)), dma((rows + 1,)),
            dma((rows - 1,)), dma((rows - 1,)),
            dma((rows - 1,)), dma((rows - 1,)),
            dma((groups - 1,)), dma((groups - 1,)),
            dma((groups,)), dma((groups,)),
            dma((groups - 1,)), dma((groups - 1,)),
            dma, dma,
        ],
        compiler_params=pltpu.CompilerParams(
            collective_id=0, has_side_effects=True, vmem_limit_bytes=60 * 1024 * 1024
        ),
    )(legendre, vectors, panel_orders, cycle_span.T, cycle_weight[None, :])


def solution(mesh):
    rows, cols = mesh.shape["row"], mesh.shape["col"]

    def body(*args):
        return per_device(rows, cols, *args)[:, None, :]

    in_specs = (P("row", "col", None), P("row", "col", None), P(), P(), P())
    return jax.shard_map(
        body, mesh=mesh, in_specs=in_specs, out_specs=P("col", "row", None), check_vma=False
    )
```

```python
import functools
import math

import jax
import jax.numpy as jnp
from jax import lax
from jax.experimental import pallas as pl
from jax.experimental.pallas import tpu as pltpu
from jax.sharding import PartitionSpec as P

NPHI = 2048
MESH = pl.DeviceIdType.MESH
BF16 = jnp.bfloat16
F32 = jnp.float32


def sine_pair(orders, cells):
    angle = (2.0 * math.pi / NPHI) * ((orders * cells) & (NPHI - 1)).astype(F32)
    return jnp.sin(angle), jnp.cos(angle)


def cycle_mix(order_of, panels, first_order, span, weight, coef_ref):
    ords, cyc = coef_ref.shape[1:]
    step = 16
    cell_angle = 2.0 * math.pi / NPHI
    start, stop = span[0:1, :], span[1:2, :]
    scale = (0.5 * cell_angle) * weight
    width = scale * (stop - start).astype(F32)
    low = lax.broadcasted_iota(jnp.int32, (step, cyc), 0)
    high_count = ords // step
    high = first_order + step * lax.broadcasted_iota(jnp.int32, (high_count, cyc), 0)
    low_stop, low_start = sine_pair(low, stop), sine_pair(low, start)
    high_stop, high_start = sine_pair(high, stop), sine_pair(high, start)
    ident = lax.broadcasted_iota(jnp.int32, (panels, cyc), 0)
    pan = jnp.zeros((panels, cyc), jnp.int32)
    for p in range(panels):
        pan = jnp.where(ident == p, order_of[p], pan)
    pan_stop = [scale * x for x in sine_pair(pan, stop)]
    pan_start = [scale * x for x in sine_pair(pan, start)]
    lane = lax.broadcasted_iota(jnp.int32, (ords, 128), 1)
    order = first_order + lax.broadcasted_iota(jnp.int32, (ords, 128), 0)
    wave = jnp.ones((ords, 128), jnp.int32)
    for p in range(panels):
        wave = jnp.where(lane == 2 * p, order_of[p] - order, wave)
        wave = jnp.where(lane == 2 * p + 1, order_of[p] + order, wave)
    zero = wave == 0
    chord = 2.0 * jnp.sin((math.pi / NPHI) * wave.astype(F32))
    inverse = jnp.where(zero, 0.0, 1.0 / jnp.where(zero, 1.0, chord))
    zeros = zero.astype(F32)
    for a in range(high_count):
        rows = slice(a * step, (a + 1) * step)

        def turned(high_pair, low_pair):
            hs, hc = high_pair[0][a:a + 1], high_pair[1][a:a + 1]
            return hs * low_pair[1] + hc * low_pair[0], hc * low_pair[1] - hs * low_pair[0]

        stop_sin, stop_cos = turned(high_stop, low_stop)
        start_sin, start_cos = turned(high_start, low_start)
        for p in range(panels):
            one = slice(p, p + 1)
            even = pan_stop[0][one] * stop_cos - pan_start[0][one] * start_cos
            odd = pan_stop[1][one] * stop_sin - pan_start[1][one] * start_sin
            gap, total = inverse[rows, 2 * p:2 * p + 1], inverse[rows, 2 * p + 1:2 * p + 2]
            flat = zeros[rows, 2 * p:2 * p + 1] + zeros[rows, 2 * p + 1:2 * p + 2]
            coef_ref[p, rows, :] = even * (total + gap) + odd * (total - gap) + flat * width


def kernel(
    rows, cols, chunk,
    t_hbm, v_hbm, order_ref, span_ref, weight_ref, out_ref,
    coef_ref, pick_ref, tbuf, vbuf, vt, acc, own, half_send, half_recv, row_send, row_recv,
    pick_recv, tm, op_send, op_recv,
    in_sem, half_ss, half_rs, row_ss, row_rs, pick_ss, pick_rs,
    tmz_ss, tmz_rs, tmp_ss, tmp_rs, op_ss, op_rs,
):
    r = lax.axis_index("row")
    c = lax.axis_index("col")
    groups = cols // 2
    core = c % 2
    group = c // 2
    partner = group * 2 + 1 - core
    ords, degs, cyc = tbuf.shape
    vecs = vbuf.shape[2]
    half = vecs // 2
    n_chunks = ords // chunk
    depth = chunk * degs

    loads = []
    for i in range(n_chunks):
        piece = pl.ds(i * chunk, chunk)
        loads.append((
            pltpu.make_async_copy(t_hbm.at[piece], tbuf.at[piece], in_sem.at[0, i]),
            pltpu.make_async_copy(v_hbm.at[piece], vbuf.at[piece], in_sem.at[1, i]),
        ))
        loads[-1][0].start()
        loads[-1][1].start()

    barrier = pltpu.get_barrier_semaphore()
    for s in range(1, rows):
        pl.semaphore_signal(barrier, inc=1, device_id=((r + s) % rows, c), device_id_type=MESH)
    for i in range(1, cols):
        pl.semaphore_signal(barrier, inc=1, device_id=(r, (c + i) % cols), device_id_type=MESH)

    def remote(src, dst, ss, rs, dev):
        copy = pltpu.make_async_remote_copy(
            src_ref=src, dst_ref=dst, send_sem=ss, recv_sem=rs, device_id=dev, device_id_type=MESH
        )
        copy.start()
        return copy

    panels = rows
    first_order, first_degree = r * ords, c * degs
    order_of = [order_ref[p] for p in range(panels)]
    cycle_mix(order_of, panels, first_order, span_ref[...], weight_ref[...], coef_ref)

    def kept(i):
        index = i * depth + lax.broadcasted_iota(jnp.int32, (16, depth), 1)
        shift = degs.bit_length() - 1
        order = first_order + lax.shift_right_logical(index, shift)
        degree = first_degree + (index & (degs - 1))
        return jnp.where(degree >= order, 1.0, 0.0).astype(BF16)[:1]

    def pick(p):
        place = jnp.clip(order_of[p] - first_order, 0, ords - 1)
        held = (order_of[p] >= first_order) & (order_of[p] < first_order + ords)
        degree = first_degree + lax.broadcasted_iota(jnp.int32, (degs, cyc), 0)
        keep = (degree >= order_of[p]) & held
        pick_ref[p] = jnp.where(keep, tbuf[place].astype(F32), 0.0).astype(BF16)

    def scaled(panel, start, count, span):
        width = cyc if span is None else cyc // 2
        span = slice(None) if span is None else span
        terms = []
        for o in range(count):
            index = start + o
            scale = jnp.broadcast_to(coef_ref[panel, pl.ds(index, 1), span], (16, width)).astype(BF16)
            block = tbuf[index, :, span].reshape(degs // 16, 16, width) * scale[None]
            terms.append(block.reshape(degs, width))
        return jnp.concatenate(terms, axis=0)

    def first_phase(panel):
        acc[...] = jnp.zeros_like(acc)
        for i in range(n_chunks):
            loads[i][0].wait()
            loads[i][1].wait()
            span = slice(i * depth, (i + 1) * depth)
            block = vbuf[i * chunk:(i + 1) * chunk].reshape(depth, vecs)
            turned = block.T * kept(i)
            vt[:, span] = turned
            acc[...] += jnp.dot(turned, scaled(panel, i * chunk, chunk, None), preferred_element_type=F32)

    def half_phase(panel, span):
        acc[:, span] = jnp.zeros((vecs, cyc // 2), F32)
        merge = 4 if ords % (4 * chunk) == 0 else 1
        large, long = merge * chunk, merge * depth

        @pl.loop(0, ords // large)
        def _(i):
            left = vt[:, pl.ds(pl.multiple_of(i * long, long), long)]
            acc[:, span] += jnp.dot(left, scaled(panel, i * large, large, span), preferred_element_type=F32)

    mine = pl.ds(pl.multiple_of(core * half, half), half)
    other = pl.ds(pl.multiple_of((1 - core) * half, half), half)
    halves = []
    rowed = []

    spans = (slice(0, cyc // 2), slice(cyc // 2, cyc))

    def send_half(s, span, sem):
        own[s, :, span] = acc[mine, span]
        half_send[s, :, span] = acc[other, span].astype(BF16)
        halves.append(
            remote(half_send.at[s, :, span], half_recv.at[s, :, span], half_ss.at[sem], half_rs.at[sem], (r, partner))
        )

    def send_row(s):
        halves[s].wait()
        row_send[s] = (own[s] + half_recv[s].astype(F32)).astype(BF16)
        rowed.append(remote(row_send.at[s], row_recv.at[s], row_ss.at[s], row_rs.at[s], ((r + s + 1) % rows, c)))

    for s in range(rows):
        panel = (r + s + 1) % rows
        if s == 0:
            first_phase(panel)
            pl.semaphore_wait(barrier, (rows - 1) + (cols - 1))
            send_half(0, slice(0, cyc), 0)
            for p in range(panels):
                pick(p)
            picks = [
                remote(pick_ref.at[(r + q) % rows], pick_recv.at[q - 1], pick_ss.at[q - 1],
                       pick_rs.at[q - 1], ((r + q) % rows, c))
                for q in range(1, rows)
            ]
            continue
        half_phase(panel, spans[0])
        send_row(s - 1)
        if s == rows - 1:
            send_half(s, spans[0], s)
        if s == 1:
            for copy in picks:
                copy.wait()
            found = pick_ref[r].astype(F32)
            for q in range(rows - 1):
                found = found + pick_recv[q].astype(F32)
            tm[c] = found.astype(BF16)
            later = [
                remote(tm.at[c], tm.at[c], tmz_ss.at[i - 1], tmz_rs.at[i - 1],
                       (r, ((group + i) % groups) * 2 + core))
                for i in range(1, groups)
            ]
            later_core = [remote(tm.at[c], tm.at[c], tmp_ss.at[0], tmp_rs.at[0], (r, partner))]
        half_phase(panel, spans[1])
        if s < rows - 1:
            send_half(s, slice(0, cyc), s)
        else:
            send_half(s, spans[1], s + 1)
        if s == 2:
            for i in range(1, groups):
                later[i - 1].wait()
                came = ((group - i + groups) % groups) * 2 + core
                later_core.append(
                    remote(tm.at[came], tm.at[came], tmp_ss.at[i], tmp_rs.at[i], (r, partner))
                )
    for copy in later_core:
        copy.wait()
    halves[rows - 1].wait()
    halves[rows].wait()
    summed = own[rows - 1] + half_recv[rows - 1].astype(F32)
    for s in range(rows - 1):
        rowed[s].wait()
        summed = summed + row_recv[s].astype(F32)
    summed = summed.astype(BF16)
    table = tm[...].reshape(cols * degs, cyc)
    product = lax.dot_general(table, summed, (((1,), (1,)), ((), ())), preferred_element_type=F32)
    op_send[...] = product.astype(BF16).reshape(cols, degs, half)
    sends = []
    for i in range(1, cols):
        to = (c + i) % cols
        sends.append(remote(op_send.at[to], op_recv.at[i - 1], op_ss.at[i - 1], op_rs.at[i - 1], (r, to)))
    near = op_send[c].astype(F32)
    far = jnp.zeros((degs, half), F32)
    for i in range(1, cols):
        sends[i - 1].wait()
        if i % 2:
            far = far + op_recv[i - 1].astype(F32)
        else:
            near = near + op_recv[i - 1].astype(F32)
    out_ref[:, mine] = near.astype(BF16)
    out_ref[:, other] = far.astype(BF16)


def per_device(rows, cols, legendre, vectors, panel_orders, cycle_span, cycle_weight):
    ords, degs, cyc = legendre.shape
    vecs = vectors.shape[2]
    panels = panel_orders.shape[0]
    assert panels == rows
    groups, half = cols // 2, vecs // 2
    chunk = 8
    while ords % chunk or (chunk * degs) % 128:
        chunk *= 2
    dma = pltpu.SemaphoreType.DMA
    vmem = pl.BlockSpec(memory_space=pltpu.VMEM)
    hbm = pl.BlockSpec(memory_space=pl.ANY)
    return pl.pallas_call(
        functools.partial(kernel, rows, cols, chunk),
        out_shape=jax.ShapeDtypeStruct((degs, vecs), BF16),
        in_specs=[hbm, hbm, pl.BlockSpec(memory_space=pltpu.SMEM), vmem, vmem],
        out_specs=vmem,
        scratch_shapes=[
            pltpu.VMEM((panels, ords, cyc), F32),
            pltpu.VMEM((panels, degs, cyc), BF16),
            pltpu.VMEM((ords, degs, cyc), BF16),
            pltpu.VMEM((ords, degs, vecs), BF16),
            pltpu.VMEM((vecs, ords * degs), BF16),
            pltpu.VMEM((vecs, cyc), F32),
            pltpu.VMEM((rows, half, cyc), F32),
            pltpu.VMEM((rows, half, cyc), BF16),
            pltpu.VMEM((rows, half, cyc), BF16),
            pltpu.VMEM((rows - 1, half, cyc), BF16),
            pltpu.VMEM((rows - 1, half, cyc), BF16),
            pltpu.VMEM((rows - 1, degs, cyc), BF16),
            pltpu.VMEM((cols, degs, cyc), BF16),
            pltpu.VMEM((cols, degs, half), BF16),
            pltpu.VMEM((cols - 1, degs, half), BF16),
            dma((2, ords // chunk)),
            dma((rows + 1,)), dma((rows + 1,)),
            dma((rows - 1,)), dma((rows - 1,)),
            dma((rows - 1,)), dma((rows - 1,)),
            dma((groups - 1,)), dma((groups - 1,)),
            dma((groups,)), dma((groups,)),
            dma((cols - 1,)), dma((cols - 1,)),
        ],
        compiler_params=pltpu.CompilerParams(
            collective_id=0, has_side_effects=True, vmem_limit_bytes=60 * 1024 * 1024
        ),
    )(legendre, vectors, panel_orders, cycle_span.T, cycle_weight[None, :])


def solution(mesh):
    rows, cols = mesh.shape["row"], mesh.shape["col"]

    def body(*args):
        return per_device(rows, cols, *args)[:, None, :]

    in_specs = (P("row", "col", None), P("row", "col", None), P(), P(), P())
    return jax.shard_map(
        body, mesh=mesh, in_specs=in_specs, out_specs=P("col", "row", None), check_vma=False
    )
```

```python
import functools
import math

import jax
import jax.numpy as jnp
from jax import lax
from jax.experimental import pallas as pl
from jax.experimental.pallas import tpu as pltpu
from jax.sharding import PartitionSpec as P

NPHI = 2048
MESH = pl.DeviceIdType.MESH
BF16 = jnp.bfloat16
F32 = jnp.float32


def sine_pair(orders, cells):
    angle = (2.0 * math.pi / NPHI) * ((orders * cells) & (NPHI - 1)).astype(F32)
    return jnp.sin(angle), jnp.cos(angle)


def cycle_mix(order_of, panels, first_order, span, weight, coef_ref):
    ords, cyc = coef_ref.shape[1:]
    step = 16
    cell_angle = 2.0 * math.pi / NPHI
    start, stop = span[0:1, :], span[1:2, :]
    scale = (0.5 * cell_angle) * weight
    width = scale * (stop - start).astype(F32)
    low = lax.broadcasted_iota(jnp.int32, (step, cyc), 0)
    high_count = ords // step
    high = first_order + step * lax.broadcasted_iota(jnp.int32, (high_count, cyc), 0)
    low_stop, low_start = sine_pair(low, stop), sine_pair(low, start)
    high_stop, high_start = sine_pair(high, stop), sine_pair(high, start)
    ident = lax.broadcasted_iota(jnp.int32, (panels, cyc), 0)
    pan = jnp.zeros((panels, cyc), jnp.int32)
    for p in range(panels):
        pan = jnp.where(ident == p, order_of[p], pan)
    pan_stop = [scale * x for x in sine_pair(pan, stop)]
    pan_start = [scale * x for x in sine_pair(pan, start)]
    lane = lax.broadcasted_iota(jnp.int32, (ords, 128), 1)
    order = first_order + lax.broadcasted_iota(jnp.int32, (ords, 128), 0)
    wave = jnp.ones((ords, 128), jnp.int32)
    for p in range(panels):
        wave = jnp.where(lane == 2 * p, order_of[p] - order, wave)
        wave = jnp.where(lane == 2 * p + 1, order_of[p] + order, wave)
    zero = wave == 0
    chord = 2.0 * jnp.sin((math.pi / NPHI) * wave.astype(F32))
    inverse = jnp.where(zero, 0.0, 1.0 / jnp.where(zero, 1.0, chord))
    zeros = zero.astype(F32)
    for a in range(high_count):
        rows = slice(a * step, (a + 1) * step)

        def turned(high_pair, low_pair):
            hs, hc = high_pair[0][a:a + 1], high_pair[1][a:a + 1]
            return hs * low_pair[1] + hc * low_pair[0], hc * low_pair[1] - hs * low_pair[0]

        stop_sin, stop_cos = turned(high_stop, low_stop)
        start_sin, start_cos = turned(high_start, low_start)
        for p in range(panels):
            one = slice(p, p + 1)
            even = pan_stop[0][one] * stop_cos - pan_start[0][one] * start_cos
            odd = pan_stop[1][one] * stop_sin - pan_start[1][one] * start_sin
            gap, total = inverse[rows, 2 * p:2 * p + 1], inverse[rows, 2 * p + 1:2 * p + 2]
            flat = zeros[rows, 2 * p:2 * p + 1] + zeros[rows, 2 * p + 1:2 * p + 2]
            coef_ref[p, rows, :] = even * (total + gap) + odd * (total - gap) + flat * width


def kernel(
    rows, cols, chunk,
    t_hbm, v_hbm, order_ref, span_ref, weight_ref, out_ref,
    coef_ref, pick_ref, tbuf, vbuf, vt, acc, own, half_send, half_recv, row_send, row_recv,
    pick_recv, tm, op_send, op_recv,
    in_sem, half_ss, half_rs, row_ss, row_rs, pick_ss, pick_rs,
    tmz_ss, tmz_rs, tmp_ss, tmp_rs, op_ss, op_rs,
):
    r = lax.axis_index("row")
    c = lax.axis_index("col")
    groups = cols // 2
    core = c % 2
    group = c // 2
    partner = group * 2 + 1 - core
    ords, degs, cyc = tbuf.shape
    vecs = vbuf.shape[2]
    half = vecs // 2
    n_chunks = ords // chunk
    depth = chunk * degs

    loads = []
    for i in range(n_chunks):
        piece = pl.ds(i * chunk, chunk)
        loads.append((
            pltpu.make_async_copy(t_hbm.at[piece], tbuf.at[piece], in_sem.at[0, i]),
            pltpu.make_async_copy(v_hbm.at[piece], vbuf.at[piece], in_sem.at[1, i]),
        ))
        loads[-1][0].start()
        loads[-1][1].start()

    barrier = pltpu.get_barrier_semaphore()
    for s in range(1, rows):
        pl.semaphore_signal(barrier, inc=1, device_id=((r + s) % rows, c), device_id_type=MESH)
    for i in range(1, cols):
        pl.semaphore_signal(barrier, inc=1, device_id=(r, (c + i) % cols), device_id_type=MESH)

    def remote(src, dst, ss, rs, dev):
        copy = pltpu.make_async_remote_copy(
            src_ref=src, dst_ref=dst, send_sem=ss, recv_sem=rs, device_id=dev, device_id_type=MESH
        )
        copy.start()
        return copy

    panels = rows
    first_order, first_degree = r * ords, c * degs
    order_of = [order_ref[p] for p in range(panels)]
    cycle_mix(order_of, panels, first_order, span_ref[...], weight_ref[...], coef_ref)

    def kept(i):
        index = i * depth + lax.broadcasted_iota(jnp.int32, (16, depth), 1)
        shift = degs.bit_length() - 1
        order = first_order + lax.shift_right_logical(index, shift)
        degree = first_degree + (index & (degs - 1))
        return jnp.where(degree >= order, 1.0, 0.0).astype(BF16)[:1]

    def pick(p):
        place = jnp.clip(order_of[p] - first_order, 0, ords - 1)
        held = (order_of[p] >= first_order) & (order_of[p] < first_order + ords)
        degree = first_degree + lax.broadcasted_iota(jnp.int32, (degs, cyc), 0)
        keep = (degree >= order_of[p]) & held
        pick_ref[p] = jnp.where(keep, tbuf[place].astype(F32), 0.0).astype(BF16)

    def scaled(panel, start, count, span):
        width = cyc if span is None else cyc // 2
        span = slice(None) if span is None else span
        terms = []
        for o in range(count):
            index = start + o
            scale = jnp.broadcast_to(coef_ref[panel, pl.ds(index, 1), span], (16, width)).astype(BF16)
            block = tbuf[index, :, span].reshape(degs // 16, 16, width) * scale[None]
            terms.append(block.reshape(degs, width))
        return jnp.concatenate(terms, axis=0)

    def first_phase(panel):
        acc[...] = jnp.zeros_like(acc)
        for i in range(n_chunks):
            loads[i][0].wait()
            loads[i][1].wait()
            span = slice(i * depth, (i + 1) * depth)
            block = vbuf[i * chunk:(i + 1) * chunk].reshape(depth, vecs)
            turned = block.T * kept(i)
            vt[:, span] = turned
            acc[...] += jnp.dot(turned, scaled(panel, i * chunk, chunk, None), preferred_element_type=F32)

    def half_phase(panel, span):
        acc[:, span] = jnp.zeros((vecs, cyc // 2), F32)
        merge = 8 if ords % (8 * chunk) == 0 else 1
        large, long = merge * chunk, merge * depth

        @pl.loop(0, ords // large)
        def _(i):
            left = vt[:, pl.ds(pl.multiple_of(i * long, long), long)]
            acc[:, span] += jnp.dot(left, scaled(panel, i * large, large, span), preferred_element_type=F32)

    mine = pl.ds(pl.multiple_of(core * half, half), half)
    other = pl.ds(pl.multiple_of((1 - core) * half, half), half)
    halves = []
    rowed = []

    spans = (slice(0, cyc // 2), slice(cyc // 2, cyc))

    def send_half(s, span, sem):
        half_send[s, :, span] = acc[other, span].astype(BF16)
        halves.append(
            remote(half_send.at[s, :, span], half_recv.at[s, :, span], half_ss.at[sem], half_rs.at[sem], (r, partner))
        )
        own[s, :, span] = acc[mine, span]

    def send_row(s):
        halves[s].wait()
        row_send[s] = (own[s] + half_recv[s].astype(F32)).astype(BF16)
        rowed.append(remote(row_send.at[s], row_recv.at[s], row_ss.at[s], row_rs.at[s], ((r + s + 1) % rows, c)))

    for s in range(rows):
        panel = (r + s + 1) % rows
        if s == 0:
            first_phase(panel)
            pl.semaphore_wait(barrier, (rows - 1) + (cols - 1))
            send_half(0, slice(0, cyc), 0)
            for p in range(panels):
                pick(p)
            picks = [
                remote(pick_ref.at[(r + q) % rows], pick_recv.at[q - 1], pick_ss.at[q - 1],
                       pick_rs.at[q - 1], ((r + q) % rows, c))
                for q in range(1, rows)
            ]
            continue
        half_phase(panel, spans[0])
        send_row(s - 1)
        if s == rows - 1:
            send_half(s, spans[0], s)
        if s == 1:
            for copy in picks:
                copy.wait()
            found = pick_ref[r].astype(F32)
            for q in range(rows - 1):
                found = found + pick_recv[q].astype(F32)
            tm[c] = found.astype(BF16)
            later = [
                remote(tm.at[c], tm.at[c], tmz_ss.at[i - 1], tmz_rs.at[i - 1],
                       (r, ((group + i) % groups) * 2 + core))
                for i in range(1, groups)
            ]
            later_core = [remote(tm.at[c], tm.at[c], tmp_ss.at[0], tmp_rs.at[0], (r, partner))]
        half_phase(panel, spans[1])
        if s < rows - 1:
            send_half(s, slice(0, cyc), s)
        else:
            send_half(s, spans[1], s + 1)
        if s == 2:
            for i in range(1, groups):
                later[i - 1].wait()
                came = ((group - i + groups) % groups) * 2 + core
                later_core.append(
                    remote(tm.at[came], tm.at[came], tmp_ss.at[i], tmp_rs.at[i], (r, partner))
                )
    for copy in later_core:
        copy.wait()
    table = tm[...].reshape(cols * degs, cyc)

    def applied(left, right):
        return lax.dot_general(left, right, (((1,), (1,)), ((), ())), preferred_element_type=F32)

    summed = own[rows - 1]
    for s in range(rows - 1):
        rowed[s].wait()
        summed = summed + row_recv[s].astype(F32)
    product = applied(table, summed.astype(BF16))
    for h, span in enumerate(spans):
        halves[rows - 1 + h].wait()
        product = product + applied(table[:, span], half_recv[rows - 1, :, span])
    op_send[...] = product.astype(BF16).reshape(cols, degs, half)
    sends = []
    for i in range(1, cols):
        to = (c + i) % cols
        sends.append(remote(op_send.at[to], op_recv.at[i - 1], op_ss.at[i - 1], op_rs.at[i - 1], (r, to)))
    near = op_send[c].astype(F32)
    far = jnp.zeros((degs, half), F32)
    for i in range(1, cols):
        sends[i - 1].wait()
        if i % 2:
            far = far + op_recv[i - 1].astype(F32)
        else:
            near = near + op_recv[i - 1].astype(F32)
    out_ref[:, mine] = near.astype(BF16)
    out_ref[:, other] = far.astype(BF16)


def per_device(rows, cols, legendre, vectors, panel_orders, cycle_span, cycle_weight):
    ords, degs, cyc = legendre.shape
    vecs = vectors.shape[2]
    panels = panel_orders.shape[0]
    assert panels == rows
    groups, half = cols // 2, vecs // 2
    chunk = 8
    while ords % chunk or (chunk * degs) % 128:
        chunk *= 2
    dma = pltpu.SemaphoreType.DMA
    vmem = pl.BlockSpec(memory_space=pltpu.VMEM)
    hbm = pl.BlockSpec(memory_space=pl.ANY)
    return pl.pallas_call(
        functools.partial(kernel, rows, cols, chunk),
        out_shape=jax.ShapeDtypeStruct((degs, vecs), BF16),
        in_specs=[hbm, hbm, pl.BlockSpec(memory_space=pltpu.SMEM), vmem, vmem],
        out_specs=vmem,
        scratch_shapes=[
            pltpu.VMEM((panels, ords, cyc), F32),
            pltpu.VMEM((panels, degs, cyc), BF16),
            pltpu.VMEM((ords, degs, cyc), BF16),
            pltpu.VMEM((ords, degs, vecs), BF16),
            pltpu.VMEM((vecs, ords * degs), BF16),
            pltpu.VMEM((vecs, cyc), F32),
            pltpu.VMEM((rows, half, cyc), F32),
            pltpu.VMEM((rows, half, cyc), BF16),
            pltpu.VMEM((rows, half, cyc), BF16),
            pltpu.VMEM((rows - 1, half, cyc), BF16),
            pltpu.VMEM((rows - 1, half, cyc), BF16),
            pltpu.VMEM((rows - 1, degs, cyc), BF16),
            pltpu.VMEM((cols, degs, cyc), BF16),
            pltpu.VMEM((cols, degs, half), BF16),
            pltpu.VMEM((cols - 1, degs, half), BF16),
            dma((2, ords // chunk)),
            dma((rows + 1,)), dma((rows + 1,)),
            dma((rows - 1,)), dma((rows - 1,)),
            dma((rows - 1,)), dma((rows - 1,)),
            dma((groups - 1,)), dma((groups - 1,)),
            dma((groups,)), dma((groups,)),
            dma((cols - 1,)), dma((cols - 1,)),
        ],
        compiler_params=pltpu.CompilerParams(
            collective_id=0, has_side_effects=True, vmem_limit_bytes=60 * 1024 * 1024
        ),
    )(legendre, vectors, panel_orders, cycle_span.T, cycle_weight[None, :])


def solution(mesh):
    rows, cols = mesh.shape["row"], mesh.shape["col"]

    def body(*args):
        return per_device(rows, cols, *args)[:, None, :]

    in_specs = (P("row", "col", None), P("row", "col", None), P(), P(), P())
    return jax.shard_map(
        body, mesh=mesh, in_specs=in_specs, out_specs=P("col", "row", None), check_vma=False
    )
```

```python
import functools
import math

import jax
import jax.numpy as jnp
from jax import lax
from jax.experimental import pallas as pl
from jax.experimental.pallas import tpu as pltpu
from jax.sharding import PartitionSpec as P

NPHI = 2048
MESH = pl.DeviceIdType.MESH
BF16 = jnp.bfloat16
F32 = jnp.float32


def sine_pair(orders, cells):
    angle = (2.0 * math.pi / NPHI) * ((orders * cells) & (NPHI - 1)).astype(F32)
    return jnp.sin(angle), jnp.cos(angle)


def cycle_mix(order_of, panels, first_order, span, weight, coef_ref):
    ords, cyc = coef_ref.shape[1:]
    step = 16
    cell_angle = 2.0 * math.pi / NPHI
    start, stop = span[0:1, :], span[1:2, :]
    scale = (0.5 * cell_angle) * weight
    width = scale * (stop - start).astype(F32)
    low = lax.broadcasted_iota(jnp.int32, (step, cyc), 0)
    high_count = ords // step
    high = first_order + step * lax.broadcasted_iota(jnp.int32, (high_count, cyc), 0)
    low_stop, low_start = sine_pair(low, stop), sine_pair(low, start)
    high_stop, high_start = sine_pair(high, stop), sine_pair(high, start)
    ident = lax.broadcasted_iota(jnp.int32, (panels, cyc), 0)
    pan = jnp.zeros((panels, cyc), jnp.int32)
    for p in range(panels):
        pan = jnp.where(ident == p, order_of[p], pan)
    pan_stop = [scale * x for x in sine_pair(pan, stop)]
    pan_start = [scale * x for x in sine_pair(pan, start)]
    lane = lax.broadcasted_iota(jnp.int32, (ords, 128), 1)
    order = first_order + lax.broadcasted_iota(jnp.int32, (ords, 128), 0)
    wave = jnp.ones((ords, 128), jnp.int32)
    for p in range(panels):
        wave = jnp.where(lane == 2 * p, order_of[p] - order, wave)
        wave = jnp.where(lane == 2 * p + 1, order_of[p] + order, wave)
    zero = wave == 0
    chord = 2.0 * jnp.sin((math.pi / NPHI) * wave.astype(F32))
    inverse = jnp.where(zero, 0.0, 1.0 / jnp.where(zero, 1.0, chord))
    zeros = zero.astype(F32)
    for a in range(high_count):
        rows = slice(a * step, (a + 1) * step)

        def turned(high_pair, low_pair):
            hs, hc = high_pair[0][a:a + 1], high_pair[1][a:a + 1]
            return hs * low_pair[1] + hc * low_pair[0], hc * low_pair[1] - hs * low_pair[0]

        stop_sin, stop_cos = turned(high_stop, low_stop)
        start_sin, start_cos = turned(high_start, low_start)
        for p in range(panels):
            one = slice(p, p + 1)
            even = pan_stop[0][one] * stop_cos - pan_start[0][one] * start_cos
            odd = pan_stop[1][one] * stop_sin - pan_start[1][one] * start_sin
            gap, total = inverse[rows, 2 * p:2 * p + 1], inverse[rows, 2 * p + 1:2 * p + 2]
            flat = zeros[rows, 2 * p:2 * p + 1] + zeros[rows, 2 * p + 1:2 * p + 2]
            coef_ref[p, rows, :] = even * (total + gap) + odd * (total - gap) + flat * width


def kernel(
    rows, cols, chunk,
    t_hbm, v_hbm, order_ref, span_ref, weight_ref, out_ref,
    coef_ref, pick_ref, tbuf, vbuf, vt, acc, own, half_send, half_recv, row_send, row_recv,
    pick_recv, tm, op_send, op_recv,
    in_sem, half_ss, half_rs, row_ss, row_rs, pick_ss, pick_rs,
    tmz_ss, tmz_rs, tmp_ss, tmp_rs, op_ss, op_rs,
):
    r = lax.axis_index("row")
    c = lax.axis_index("col")
    groups = cols // 2
    core = c % 2
    group = c // 2
    partner = group * 2 + 1 - core
    ords, degs, cyc = tbuf.shape
    vecs = vbuf.shape[2]
    half = vecs // 2
    n_chunks = ords // chunk
    depth = chunk * degs

    loads = []
    for i in range(n_chunks):
        piece = pl.ds(i * chunk, chunk)
        loads.append((
            pltpu.make_async_copy(t_hbm.at[piece], tbuf.at[piece], in_sem.at[0, i]),
            pltpu.make_async_copy(v_hbm.at[piece], vbuf.at[piece], in_sem.at[1, i]),
        ))
        loads[-1][0].start()
        loads[-1][1].start()

    barrier = pltpu.get_barrier_semaphore()
    for s in range(1, rows):
        pl.semaphore_signal(barrier, inc=1, device_id=((r + s) % rows, c), device_id_type=MESH)
    for i in range(1, cols):
        pl.semaphore_signal(barrier, inc=1, device_id=(r, (c + i) % cols), device_id_type=MESH)

    def remote(src, dst, ss, rs, dev):
        copy = pltpu.make_async_remote_copy(
            src_ref=src, dst_ref=dst, send_sem=ss, recv_sem=rs, device_id=dev, device_id_type=MESH
        )
        copy.start()
        return copy

    panels = rows
    first_order, first_degree = r * ords, c * degs
    order_of = [order_ref[p] for p in range(panels)]
    cycle_mix(order_of, panels, first_order, span_ref[...], weight_ref[...], coef_ref)

    def kept(i):
        index = i * depth + lax.broadcasted_iota(jnp.int32, (16, depth), 1)
        shift = degs.bit_length() - 1
        order = first_order + lax.shift_right_logical(index, shift)
        degree = first_degree + (index & (degs - 1))
        return jnp.where(degree >= order, 1.0, 0.0).astype(BF16)[:1]

    def pick(p):
        place = jnp.clip(order_of[p] - first_order, 0, ords - 1)
        held = (order_of[p] >= first_order) & (order_of[p] < first_order + ords)
        degree = first_degree + lax.broadcasted_iota(jnp.int32, (degs, cyc), 0)
        keep = (degree >= order_of[p]) & held
        pick_ref[p] = jnp.where(keep, tbuf[place].astype(F32), 0.0).astype(BF16)

    def scaled(panel, start, count, span):
        width = cyc if span is None else cyc // 2
        span = slice(None) if span is None else span
        terms = []
        for o in range(count):
            index = start + o
            scale = jnp.broadcast_to(coef_ref[panel, pl.ds(index, 1), span], (16, width)).astype(BF16)
            block = tbuf[index, :, span].reshape(degs // 16, 16, width) * scale[None]
            terms.append(block.reshape(degs, width))
        return jnp.concatenate(terms, axis=0)

    def first_phase(panel):
        acc[...] = jnp.zeros_like(acc)
        for i in range(n_chunks):
            loads[i][0].wait()
            loads[i][1].wait()
            span = slice(i * depth, (i + 1) * depth)
            block = vbuf[i * chunk:(i + 1) * chunk].reshape(depth, vecs)
            turned = block.T * kept(i)
            vt[:, span] = turned
            acc[...] += jnp.dot(turned, scaled(panel, i * chunk, chunk, None), preferred_element_type=F32)

    def half_phase(panel, span):
        acc[:, span] = jnp.zeros((vecs, cyc // 2), F32)
        merge = 8 if ords % (8 * chunk) == 0 else 1
        large, long = merge * chunk, merge * depth

        @pl.loop(0, ords // large)
        def _(i):
            left = vt[:, pl.ds(pl.multiple_of(i * long, long), long)]
            acc[:, span] += jnp.dot(left, scaled(panel, i * large, large, span), preferred_element_type=F32)

    mine = pl.ds(pl.multiple_of(core * half, half), half)
    other = pl.ds(pl.multiple_of((1 - core) * half, half), half)
    halves = []
    rowed = []

    offsets = [q for q in range(1, rows) if q != rows // 2] + [rows // 2, 0]
    spans = (slice(0, cyc // 2), slice(cyc // 2, cyc))

    def send_half(s, span, sem):
        half_send[s, :, span] = acc[other, span].astype(BF16)
        halves.append(
            remote(half_send.at[s, :, span], half_recv.at[s, :, span], half_ss.at[sem], half_rs.at[sem], (r, partner))
        )
        own[s, :, span] = acc[mine, span]

    def send_row(s):
        halves[s].wait()
        row_send[s] = (own[s] + half_recv[s].astype(F32)).astype(BF16)
        rowed.append(remote(row_send.at[s], row_recv.at[s], row_ss.at[s], row_rs.at[s], ((r + offsets[s]) % rows, c)))

    for s in range(rows):
        panel = (r + offsets[s]) % rows
        if s == 0:
            first_phase(panel)
            pl.semaphore_wait(barrier, (rows - 1) + (cols - 1))
            send_half(0, slice(0, cyc), 0)
            for p in range(panels):
                pick(p)
            picks = [
                remote(pick_ref.at[(r + q) % rows], pick_recv.at[q - 1], pick_ss.at[q - 1],
                       pick_rs.at[q - 1], ((r + q) % rows, c))
                for q in range(1, rows)
            ]
            continue
        half_phase(panel, spans[0])
        send_row(s - 1)
        if s == rows - 1:
            send_half(s, spans[0], s)
        if s == 1:
            for copy in picks:
                copy.wait()
            found = pick_ref[r].astype(F32)
            for q in range(rows - 1):
                found = found + pick_recv[q].astype(F32)
            tm[c] = found.astype(BF16)
            later = [
                remote(tm.at[c], tm.at[c], tmz_ss.at[i - 1], tmz_rs.at[i - 1],
                       (r, ((group + i) % groups) * 2 + core))
                for i in range(1, groups)
            ]
            later_core = [remote(tm.at[c], tm.at[c], tmp_ss.at[0], tmp_rs.at[0], (r, partner))]
        half_phase(panel, spans[1])
        if s < rows - 1:
            send_half(s, slice(0, cyc), s)
        else:
            send_half(s, spans[1], s + 1)
        if s == 2:
            for i in range(1, groups):
                later[i - 1].wait()
                came = ((group - i + groups) % groups) * 2 + core
                later_core.append(
                    remote(tm.at[came], tm.at[came], tmp_ss.at[i], tmp_rs.at[i], (r, partner))
                )
    for copy in later_core:
        copy.wait()
    table = tm[...].reshape(cols * degs, cyc)

    def applied(left, right):
        return lax.dot_general(left, right, (((1,), (1,)), ((), ())), preferred_element_type=F32)

    summed = own[rows - 1]
    for s in range(rows - 1):
        rowed[s].wait()
        summed = summed + row_recv[s].astype(F32)
    product = applied(table, summed.astype(BF16))
    for h, span in enumerate(spans):
        halves[rows - 1 + h].wait()
        product = product + applied(table[:, span], half_recv[rows - 1, :, span])
    op_send[...] = product.astype(BF16).reshape(cols, degs, half)
    sends = []
    for i in range(1, cols):
        to = (c + i) % cols
        sends.append(remote(op_send.at[to], op_recv.at[i - 1], op_ss.at[i - 1], op_rs.at[i - 1], (r, to)))
    near = op_send[c].astype(F32)
    far = jnp.zeros((degs, half), F32)
    for i in range(1, cols):
        sends[i - 1].wait()
        if i % 2:
            far = far + op_recv[i - 1].astype(F32)
        else:
            near = near + op_recv[i - 1].astype(F32)
    out_ref[:, mine] = near.astype(BF16)
    out_ref[:, other] = far.astype(BF16)


def per_device(rows, cols, legendre, vectors, panel_orders, cycle_span, cycle_weight):
    ords, degs, cyc = legendre.shape
    vecs = vectors.shape[2]
    panels = panel_orders.shape[0]
    assert panels == rows
    groups, half = cols // 2, vecs // 2
    chunk = 8
    while ords % chunk or (chunk * degs) % 128:
        chunk *= 2
    dma = pltpu.SemaphoreType.DMA
    vmem = pl.BlockSpec(memory_space=pltpu.VMEM)
    hbm = pl.BlockSpec(memory_space=pl.ANY)
    return pl.pallas_call(
        functools.partial(kernel, rows, cols, chunk),
        out_shape=jax.ShapeDtypeStruct((degs, vecs), BF16),
        in_specs=[hbm, hbm, pl.BlockSpec(memory_space=pltpu.SMEM), vmem, vmem],
        out_specs=vmem,
        scratch_shapes=[
            pltpu.VMEM((panels, ords, cyc), F32),
            pltpu.VMEM((panels, degs, cyc), BF16),
            pltpu.VMEM((ords, degs, cyc), BF16),
            pltpu.VMEM((ords, degs, vecs), BF16),
            pltpu.VMEM((vecs, ords * degs), BF16),
            pltpu.VMEM((vecs, cyc), F32),
            pltpu.VMEM((rows, half, cyc), F32),
            pltpu.VMEM((rows, half, cyc), BF16),
            pltpu.VMEM((rows, half, cyc), BF16),
            pltpu.VMEM((rows - 1, half, cyc), BF16),
            pltpu.VMEM((rows - 1, half, cyc), BF16),
            pltpu.VMEM((rows - 1, degs, cyc), BF16),
            pltpu.VMEM((cols, degs, cyc), BF16),
            pltpu.VMEM((cols, degs, half), BF16),
            pltpu.VMEM((cols - 1, degs, half), BF16),
            dma((2, ords // chunk)),
            dma((rows + 1,)), dma((rows + 1,)),
            dma((rows - 1,)), dma((rows - 1,)),
            dma((rows - 1,)), dma((rows - 1,)),
            dma((groups - 1,)), dma((groups - 1,)),
            dma((groups,)), dma((groups,)),
            dma((cols - 1,)), dma((cols - 1,)),
        ],
        compiler_params=pltpu.CompilerParams(
            collective_id=0, has_side_effects=True, vmem_limit_bytes=60 * 1024 * 1024
        ),
    )(legendre, vectors, panel_orders, cycle_span.T, cycle_weight[None, :])


def solution(mesh):
    rows, cols = mesh.shape["row"], mesh.shape["col"]

    def body(*args):
        return per_device(rows, cols, *args)[:, None, :]

    in_specs = (P("row", "col", None), P("row", "col", None), P(), P(), P())
    return jax.shard_map(
        body, mesh=mesh, in_specs=in_specs, out_specs=P("col", "row", None), check_vma=False
    )
```
